128 devices in a mesh: dom: 16 (over z, x), band: 8 (over y, core).
Axes of the slice: x: 4, y: 4, z: 4, core: 2. Of those that a mesh axis runs over, the one named last changes fastest.
Arguments:
- orbitals: float32 [2560, 32, 8, 128], P('band', 'dom'), may hold values from -12 to 12, as said below
- potential: float32 [32, 8, 128], P('dom'), may hold values from -2 to 0
Outputs:
- filtered: float32 [2560, 32, 8, 128], P('band', 'dom')
The draws below stay inside these ranges and needn't reach their ends.
Inputs may be any that keep to these rules, and one draw needn't show every extreme that they name: real-valued orbitals.
All inputs are finite; a program needn't handle non-finite values.
Results may differ from the reference program's by a relative error of at most 0.00029.
Values sent between devices are 32-bit elements; how exact they have to be, the bound alone decides.
A program may use at most 192 MiB of HBM per device.

```python
import jax
import jax.numpy as jnp
from jax import lax

ORB_DEV = 320
PANEL = 64
PANELS = 3
NS_ITERS = 16
CY = 8
CZ = 128
NORB = 2560
NX = 32
N_BAND = 8


def draw_orbitals(key, part):
    key_base = jax.random.fold_in(key, 11)
    key_common = jax.random.fold_in(key, 12)
    key_weight = jax.random.fold_in(key, 13)
    common = jnp.clip(jax.random.normal(key_common, (NX, CY, CZ), jnp.float32), -5.0, 5.0)
    weights = jax.random.uniform(key_weight, (NORB, 1, 1, 1), jnp.float32, 0.3, 1.0)
    base = jnp.clip(jax.random.normal(key_base, (NORB, NX, CY, CZ), jnp.float32), -5.0, 5.0)
    return base + weights * common


def shard_levels(own_key, dims, cuts, low, high):
    def one(dim, blocks):
        steps = jax.random.uniform(jax.random.fold_in(jax.random.fold_in(own_key, 6), dim), (blocks,), jnp.float32, low / len(cuts), high / len(cuts))
        return jnp.repeat(jnp.exp(steps), dims[dim] // blocks).reshape((-1,) + (1,) * (len(dims) - dim - 1))

    loudness = one(*cuts[0])
    for cut in cuts[1:]:
        loudness = loudness * one(*cut)
    return loudness


def setup_inputs(seed: int = 0) -> dict:
    splits = jax.random.split(jax.random.key(seed), 3)
    orbitals = draw_orbitals(jax.random.fold_in(splits[2], 71), 0)
    potential = jnp.clip(-2.0 + 2.0 * jax.random.uniform(splits[1], (NX, CY, CZ), jnp.float32) ** shard_levels(splits[1], (NX, CY, CZ), ((0, 16),), -0.2, 0.2), -2.0, 0.0)
    return {"orbitals": orbitals, "potential": potential}


SHIFT = 1.0
HALF = 1.5

def hdot(left, right):
    return jnp.dot(left, right, precision=lax.Precision.HIGHEST, preferred_element_type=jnp.float32)

def rolled(values, offset, which):
    return jnp.roll(values, offset, axis=which)

def apply_h(field_pad, potential_pad):
    centre = field_pad[:, 1:-1]
    upper = field_pad[:, 2:]
    lower = field_pad[:, :-2]
    face_sum = upper + lower + rolled(centre, 1, 2) + rolled(centre, -1, 2) + rolled(centre, 1, 3) + rolled(centre, -1, 3)
    edge_sum = jnp.zeros_like(centre)
    for offset in (1, -1):
        edge_sum = edge_sum + rolled(upper, offset, 2) + rolled(lower, offset, 2) + rolled(upper, offset, 3) + rolled(lower, offset, 3)
        for second in (1, -1):
            edge_sum = edge_sum + rolled(rolled(centre, offset, 2), second, 3)
    laplace = (2.0 * face_sum + edge_sum - 24.0 * centre) / 6.0
    weighted = potential_pad[None] * field_pad
    middle = weighted[:, 1:-1]
    near_sum = weighted[:, 2:] + weighted[:, :-2] + rolled(middle, 1, 2) + rolled(middle, -1, 2) + rolled(middle, 1, 3) + rolled(middle, -1, 3)
    return -0.5 * laplace + 0.5 * middle + near_sum / 12.0

def inv_sqrt(correlation):
    order = correlation.shape[0]
    eye = jnp.eye(order, dtype=jnp.float32)
    scale = jnp.sqrt(jnp.sum(correlation * correlation))
    root = correlation / scale
    inverse = eye
    for turn in range(NS_ITERS):
        factor = 0.5 * (3.0 * eye - hdot(inverse, root))
        root = hdot(root, factor)
        inverse = hdot(factor, inverse)
    return inverse / jnp.sqrt(scale)

def reference(orbitals, potential):
    potential_pad = jnp.concatenate([potential[-1:], potential, potential[:1]], axis=0)

    def filter_block(block):
        padded = jnp.concatenate([block[:, -1:], block, block[:, :1]], axis=1)
        first = (apply_h(padded, potential_pad) - SHIFT * block) / HALF
        padded_first = jnp.concatenate([first[:, -1:], first, first[:, :1]], axis=1)
        return 2.0 * (apply_h(padded_first, potential_pad) - SHIFT * first) / HALF - block
    grouped = orbitals.reshape(N_BAND, ORB_DEV, NX, CY, CZ)
    swept = lax.map(filter_block, grouped)
    blocks = [swept[index].reshape(ORB_DEV, NX * CY * CZ) for index in range(N_BAND)]
    local_row = jnp.arange(ORB_DEV)
    for panel_index in range(PANELS):
        panel = blocks[panel_index][:PANEL]
        weights = inv_sqrt(hdot(panel, panel.T))
        basis = hdot(weights, panel)
        for index in range(N_BAND):
            coeffs = hdot(basis, blocks[index].T)
            if index <= panel_index:
                keep = jnp.where(local_row < PANEL, 0.0, 1.0).astype(jnp.float32)
            else:
                keep = jnp.ones((ORB_DEV,), jnp.float32)
            updated = blocks[index] - keep[:, None] * hdot(coeffs.T, basis)
            if index == panel_index:
                updated = updated.at[:PANEL].set(basis)
            blocks[index] = updated
    return jnp.stack(blocks).reshape(NORB, NX, CY, CZ)
```

```python
import jax
import jax.numpy as jnp
from jax import lax
from jax.experimental import pallas as pl
from jax.experimental.pallas import tpu as pltpu
from jax.sharding import PartitionSpec as P

PANEL = 64
PANELS = 3
NS_ITERS = 16
ROWS = 320
DOM = 16
BAND = 8
ALL = PANEL * PANELS
CUTS = (0, 32, 64, 128, 192, 224, 256, 288, 320)
CHUNKS = tuple((a, b - a) for a, b in zip(CUTS, CUTS[1:]))
EARLY = 5
MESH = pl.DeviceIdType.MESH
F32 = jnp.float32
BF16 = jnp.bfloat16


def pieces(value, count):
    out = []
    for _ in range(count - 1):
        head = value.astype(BF16)
        out.append(head)
        value = value - head.astype(F32)
    out.append(value.astype(BF16))
    return out


def mm(left, right):
    return jnp.dot(left, right, preferred_element_type=F32)


def mm_t(left, right):
    return lax.dot_general(left, right, (((1,), (1,)), ((), ())), preferred_element_type=F32)


def exact(left, right):
    a0, a1, a2 = pieces(left, 3)
    b0, b1, b2 = pieces(right, 3)
    a = jnp.concatenate([a0, a0, a1, a0, a2, a1], axis=1)
    b = jnp.concatenate([b0, b1, b0, b2, b0, b1], axis=0)
    return mm(a, b)


def exact_in_two(left, right):
    a0, a1, a2 = pieces(left, 3)
    b0, b1, b2 = pieces(right, 3)
    large = mm(jnp.concatenate([a0, a0, a1], axis=1), jnp.concatenate([b0, b1, b0], axis=0))
    return large + mm(jnp.concatenate([a0, a2, a1], axis=1), jnp.concatenate([b2, b0, b1], axis=0))


def exact_t(left, right):
    a0, a1, a2 = pieces(left, 3)
    b0, b1, b2 = pieces(right, 3)
    a = jnp.concatenate([a0, a0, a1, a0, a2, a1], axis=1)
    b = jnp.concatenate([b0, b1, b0, b2, b0, b1], axis=1)
    return mm_t(a, b)


def identity(order):
    row = lax.broadcasted_iota(jnp.int32, (order, order), 0)
    return (row == lax.broadcasted_iota(jnp.int32, (order, order), 1)).astype(F32)


def inv_sqrt(correlation):
    eye = identity(PANEL)
    scale = jnp.sqrt(jnp.sum(correlation * correlation, keepdims=True))

    def turn(_, carry):
        root, inverse = carry
        factor = 0.5 * (3.0 * eye - exact_in_two(inverse, root))
        return exact_in_two(root, factor), exact_in_two(factor, inverse)

    _, inverse = lax.fori_loop(0, NS_ITERS, turn, (correlation / scale, eye))
    return inverse / jnp.sqrt(scale)


def around(value, axis):
    return pltpu.roll(value, 1, axis) + pltpu.roll(value, value.shape[axis] - 1, axis)


def twelve_h(field, weighted, j):
    v, w = field[j], weighted[j]
    outer = field[j - 1] + field[j + 1]
    part = w - 2.0 * v - outer
    near = weighted[j - 1] + weighted[j + 1]
    return 24.0 * v + 6.0 * w - 2.0 * outer + near + around(part, 0) + around(part - around(v, 0), 1)


def filtered(v, pot):
    w = [a * b for a, b in zip(v, pot)]
    first = [None] + [twelve_h(v, w, j) * (1.0 / 18.0) - v[j] * (2.0 / 3.0) for j in range(1, 5)] + [None]
    w = [None] + [first[j] * pot[j] for j in range(1, 5)] + [None]
    return [twelve_h(first, w, j) * (1.0 / 9.0) - first[j] * (4.0 / 3.0) - v[j] for j in (2, 3)]


class Sum:
    def __init__(self, refs, rows, dom):
        self.loc, self.zin, self.part, self.xin, self.full, self.send, self.recv = refs
        self.n = rows // 4
        self.z = dom // 4
        self.x = lax.rem(dom, 4)
        self.zs = [lax.rem(self.z + k, 4) for k in (1, 2, 3)]
        self.xs = [lax.rem(self.x + k, 4) for k in (1, 2, 3)]

    def block(self, ref, z):
        return ref.at[pl.ds(pl.multiple_of(z * self.n, 8), self.n)]

    def copies(self, phase):
        out = []
        for k in range(3):
            if phase == 0:
                src, dst = self.block(self.loc, self.zs[k]), self.zin.at[k]
            elif phase == 1:
                src, dst = self.part, self.xin.at[k]
            else:
                src = dst = self.block(self.full, self.z)
            to = self.z * 4 + self.xs[k] if phase == 1 else self.zs[k] * 4 + self.x
            out.append(
                pltpu.make_async_remote_copy(
                    src_ref=src,
                    dst_ref=dst,
                    send_sem=self.send.at[phase, k],
                    recv_sem=self.recv.at[phase, k],
                    device_id={"dom": to},
                    device_id_type=MESH,
                )
            )
        return out

    def start(self):
        for copy in self.copies(0):
            copy.start()

    def over_z(self):
        for copy in self.copies(0):
            copy.wait_recv()
        mine = self.block(self.loc, self.z)
        self.part[...] = mine[...] + self.zin[0] + self.zin[1] + self.zin[2]
        for copy in self.copies(1):
            copy.start()

    def over_x(self):
        for copy in self.copies(1):
            copy.wait_recv()
        mine = self.block(self.full, self.z)
        mine[...] = self.part[...] + self.xin[0] + self.xin[1] + self.xin[2]
        for copy in self.copies(2):
            copy.start()

    def end(self):
        for copy in self.copies(2):
            copy.wait_recv()

    def sent(self):
        for phase in range(3):
            for copy in self.copies(phase):
                copy.wait_send()


def sum_scratch(rows):
    n = rows // 4
    return [
        pltpu.VMEM((rows, ALL), F32),
        pltpu.VMEM((3, n, ALL), F32),
        pltpu.VMEM((n, ALL), F32),
        pltpu.VMEM((3, n, ALL), F32),
        pltpu.VMEM((rows, ALL), F32),
        pltpu.SemaphoreType.DMA((3, 3)),
        pltpu.SemaphoreType.DMA((3, 3)),
    ]


BULK = 256


def body(orb, pot, y_out, p_out, d_out, own, left_in, right_in, pots, ym, pm, ph, plo, *rest):
    sums, sems = rest[:21], rest[21:]
    halo_s, halo_r, pot_s, pot_r, pan_s, pan_r, relay_s, local = sems
    dom, band = lax.axis_index("dom"), lax.axis_index("band")
    core, y = lax.rem(band, 2), band // 2
    right, left = lax.rem(dom + 1, DOM), lax.rem(dom + DOM - 1, DOM)
    gram = Sum(sums[:7], ALL, dom)
    bulk = Sum(sums[7:14], BULK, dom)
    last = Sum(sums[14:], ROWS - BULK, dom)

    barrier = pltpu.get_barrier_semaphore()
    peers = [{"dom": right}, {"dom": left}]
    peers += [{"dom": z * 4 + gram.x} for z in gram.zs] + [{"dom": gram.z * 4 + x} for x in gram.xs]
    peers += [{"band": lax.rem(band + k, BAND)} for k in range(1, BAND)]
    for peer in peers:
        pl.semaphore_signal(barrier, inc=1, device_id=peer, device_id_type=MESH)
    pl.semaphore_wait(barrier, len(peers))

    def remote(src, dst, send, recv, device):
        return pltpu.make_async_remote_copy(
            src_ref=src, dst_ref=dst, send_sem=send, recv_sem=recv, device_id=device, device_id_type=MESH
        )

    def halo(c):
        rows = pl.ds(*CHUNKS[c])
        return [
            remote(orb.at[rows], left_in.at[rows], halo_s.at[0, c], halo_r.at[0, c], {"dom": right}),
            remote(orb.at[rows], right_in.at[rows], halo_s.at[1, c], halo_r.at[1, c], {"dom": left}),
        ]

    def pot_halo():
        return [
            remote(pot, pots.at[0], pot_s.at[0], pot_r.at[0], {"dom": right}),
            remote(pot, pots.at[2], pot_s.at[1], pot_r.at[1], {"dom": left}),
        ]

    for copy in pot_halo():
        copy.start()
    for c in range(EARLY):
        for copy in halo(c):
            copy.start()
    mine = [pltpu.make_async_copy(orb, own, local.at[0]), pltpu.make_async_copy(pot, pots.at[1], local.at[1])]
    for copy in mine:
        copy.start()
    for copy in mine:
        copy.wait()
    for copy in pot_halo():
        copy.wait_recv()

    flat = ym.reshape(16 * ROWS, 128)

    def run_filter(c):
        begin, count = CHUNKS[c]
        for copy in halo(c):
            copy.wait_recv()
        potential = [pots[j // 2, j % 2] for j in range(6)]

        def some(i, _):
            for step in range(2):
                o = begin + 2 * i + step
                v = [left_in[o, 0], left_in[o, 1], own[o, 0], own[o, 1], right_in[o, 0], right_in[o, 1]]
                for plane, value in enumerate(filtered(v, potential)):
                    flat[pl.ds(plane * 8 * ROWS + o, 8, stride=ROWS), :] = value
            return 0

        lax.fori_loop(0, count // 2, some, 0)

    def y_copy(c):
        rows = pl.ds(*CHUNKS[c])
        return pltpu.make_async_copy(ym.at[:, rows], y_out.at[:, rows], local.at[2 + c])

    def panel_rows(p, half):
        return pm.at[:, pl.ds(p * PANEL + half * 32, 32)]

    def owner_copies(p, half):
        rows = ym.at[:, pl.ds(half * 32, 32)]
        targets = [p ^ 1, (p + 2) % BAND, (p + 4) % BAND, (p + 6) % BAND]
        return [
            remote(rows, panel_rows(p, half), pan_s.at[half, k], pan_r.at[p, half], {"band": t})
            for k, t in enumerate(targets)
        ]

    def relay_copy(p, half):
        ref = panel_rows(p, half)
        return remote(ref, ref, relay_s.at[p, half], pan_r.at[p, half], {"band": band + 1 - 2 * core})

    def relays(p):
        return (core == p % 2) & (y != p // 2)

    def send_panel(half):
        for p in range(PANELS):

            @pl.when(band == p)
            def _():
                for copy in owner_copies(p, half):
                    copy.start()
                begin, count = CHUNKS[half]
                pm[:, p * PANEL + begin : p * PANEL + begin + count] = ym[:, begin : begin + count]

    def take_panel(half):
        for p in range(PANELS):

            @pl.when(band != p)
            def _():
                relay_copy(p, half).wait_recv()

            @pl.when(relays(p))
            def _():
                relay_copy(p, half).start()

    def inner(c, total, at):
        begin, count = CHUNKS[c]

        def some(k, acc):
            a0, a1 = pieces(ym[k, begin : begin + count], 2)
            b0, b1 = ph[k], plo[k]
            return acc + (mm_t(a0, b0) + (mm_t(a0, b1) + mm_t(a1, b0)))

        total.loc[at : at + count] = lax.fori_loop(0, 16, some, jnp.zeros((count, ALL), F32))

    run_filter(0)
    send_panel(0)
    run_filter(1)
    send_panel(1)
    take_panel(0)
    run_filter(2)
    y_copy(2).start()
    take_panel(1)

    p_copy = pltpu.make_async_copy(pm, p_out, local.at[2 + len(CHUNKS)])
    p_copy.start()

    def gram_step(k, acc):
        a0, a1 = pieces(pm[k], 2)
        ph[k] = a0
        plo[k] = a1
        return acc + (mm_t(a0, a0) + (mm_t(a0, a1) + mm_t(a1, a0)))

    gram.loc[...] = lax.fori_loop(0, 16, gram_step, jnp.zeros((ALL, ALL), F32))
    gram.start()
    inner(0, bulk, 0)
    inner(1, bulk, 32)
    inner(2, bulk, 64)
    gram.over_z()
    for c in range(EARLY, len(CHUNKS)):
        for copy in halo(c):
            copy.start()
    for half in range(2):
        for p in range(PANELS):

            @pl.when(band == p)
            def _():
                for copy in owner_copies(p, half):
                    copy.wait_send()
                begin, count = CHUNKS[half]
                ym[:, begin : begin + count] = jnp.zeros((16, count, 128), F32)

        y_copy(half).start()
    run_filter(3)
    y_copy(3).start()
    inner(3, bulk, 128)
    gram.over_x()
    run_filter(4)
    y_copy(4).start()
    inner(4, bulk, 192)
    gram.end()

    g = gram.full[...]
    eye = identity(PANEL)
    none = jnp.zeros((PANEL, PANEL), F32)
    t0 = jnp.concatenate([inv_sqrt(g[:PANEL, :PANEL]), none, none], axis=1)
    t0g = exact(t0, g)
    a = jnp.concatenate([jnp.concatenate([none, eye, none], axis=1), jnp.concatenate([none, none, eye], axis=1)], axis=0)
    a = a - exact(exact_t(g[PANEL:], t0), t0)
    ag = exact(a, g)
    s1 = exact_t(ag[:PANEL], a[:PANEL])
    run_filter(5)
    y_copy(5).start()
    inner(5, bulk, 224)
    bulk.start()
    t1 = exact(inv_sqrt(s1), a[:PANEL])
    t1g = exact(t1, g)
    a = a[PANEL:] - exact(exact_t(ag[PANEL:], t1), t1)
    s2 = exact_t(exact(a, g), a)
    bulk.over_z()
    run_filter(6)
    y_copy(6).start()
    inner(6, last, 0)
    run_filter(7)
    y_copy(7).start()
    inner(7, last, 32)
    last.start()
    t2 = exact(inv_sqrt(s2), a)
    bulk.over_x()
    last.over_z()
    t2g = exact(t2, g)
    r0 = t0
    r1 = t1 - exact(exact_t(t1g, t0), r0)
    r2 = t2 - exact(exact_t(t2g, t0), r0) - exact(exact_t(t2g, t1), r1)
    t = jnp.concatenate([t0, t1, t2], axis=0)
    r = jnp.concatenate([r0, r1, r2], axis=0)
    bulk.end()
    last.over_x()
    d_out[:BULK] = exact(exact_t(bulk.full[...], r), t)
    for p, rows in enumerate((t0, t1, t2)):

        @pl.when(band == p)
        def _():
            d_out[:PANEL] = -rows

    last.end()
    d_out[BULK:] = exact(exact_t(last.full[...], r), t)

    for c in range(len(CHUNKS)):
        for copy in halo(c):
            copy.wait_send()
        y_copy(c).wait()
    for copy in pot_halo():
        copy.wait_send()
    for half in range(2):
        for p in range(PANELS):

            @pl.when(relays(p))
            def _():
                relay_copy(p, half).wait_send()

    p_copy.wait()
    for total in (gram, bulk, last):
        total.sent()


def project(orb, pot):
    scratch = [pltpu.VMEM((ROWS, 2, 8, 128), F32)] * 3 + [
        pltpu.VMEM((3, 2, 8, 128), F32),
        pltpu.VMEM((16, ROWS, 128), F32),
        pltpu.VMEM((16, ALL, 128), F32),
        pltpu.VMEM((16, ALL, 128), BF16),
        pltpu.VMEM((16, ALL, 128), BF16),
    ]
    scratch += sum_scratch(ALL) + sum_scratch(BULK) + sum_scratch(ROWS - BULK)
    scratch += [
        pltpu.SemaphoreType.DMA((2, len(CHUNKS))),
        pltpu.SemaphoreType.DMA((2, len(CHUNKS))),
        pltpu.SemaphoreType.DMA((2,)),
        pltpu.SemaphoreType.DMA((2,)),
        pltpu.SemaphoreType.DMA((2, 4)),
        pltpu.SemaphoreType.DMA((PANELS, 2)),
        pltpu.SemaphoreType.DMA((PANELS, 2)),
        pltpu.SemaphoreType.DMA((3 + len(CHUNKS),)),
    ]
    anywhere = pl.BlockSpec(memory_space=pl.ANY)
    return pl.pallas_call(
        body,
        out_shape=(
            jax.ShapeDtypeStruct((16, ROWS, 128), F32),
            jax.ShapeDtypeStruct((16, ALL, 128), F32),
            jax.ShapeDtypeStruct((ROWS, ALL), F32),
        ),
        in_specs=[anywhere, anywhere],
        out_specs=(anywhere, anywhere, pl.BlockSpec(memory_space=pltpu.VMEM)),
        scratch_shapes=scratch,
        compiler_params=pltpu.CompilerParams(collective_id=0, has_side_effects=True, vmem_limit_bytes=40 << 20),
        name="filter_and_project",
    )(orb, pot)


STEP = 64


def update_body(y, p, d, out, ph, plo):
    @pl.when(pl.program_id(0) == 0)
    def _():
        def cast(k, _):
            ph[k], plo[k] = pieces(p[k], 2)
            return 0

        lax.fori_loop(0, 16, cast, 0)

    d0, d1 = pieces(d[...], 2)
    flat = out.reshape(STEP * 16, 128)

    def some(k, _):
        rows = y[k] - (mm(d0, ph[k]) + (mm(d0, plo[k]) + mm(d1, ph[k])))
        for i in range(STEP // 8):
            flat[pl.ds(i * 128 + k, 8, stride=16), :] = rows[i * 8 : i * 8 + 8]
        return 0

    lax.fori_loop(0, 16, some, 0)


def update(y, p, d):
    return pl.pallas_call(
        update_body,
        grid=(ROWS // STEP,),
        out_shape=jax.ShapeDtypeStruct((ROWS, 2, 8, 128), F32),
        in_specs=[
            pl.BlockSpec((16, STEP, 128), lambda i: (0, i, 0)),
            pl.BlockSpec((16, ALL, 128), lambda i: (0, 0, 0), pipeline_mode=pl.Buffered(1)),
            pl.BlockSpec((STEP, ALL), lambda i: (i, 0)),
        ],
        out_specs=pl.BlockSpec((STEP, 2, 8, 128), lambda i: (i, 0, 0, 0)),
        scratch_shapes=[pltpu.VMEM((16, ALL, 128), BF16), pltpu.VMEM((16, ALL, 128), BF16)],
        compiler_params=pltpu.CompilerParams(vmem_limit_bytes=24 << 20),
        name="apply_update",
    )(y, p, d)


def per_device(orbitals, potential):
    return update(*project(orbitals, potential))


def solution(mesh):
    spec = P("band", "dom", None, None)
    return jax.shard_map(
        per_device, mesh=mesh, in_specs=(spec, P("dom", None, None)), out_specs=spec, check_vma=False
    )
```

```python
import jax
import jax.numpy as jnp
from jax import lax
from jax.experimental import pallas as pl
from jax.experimental.pallas import tpu as pltpu
from jax.sharding import PartitionSpec as P

PANEL = 64
PANELS = 3
NS_ITERS = 16
ROWS = 320
DOM = 16
BAND = 8
ALL = PANEL * PANELS
CUTS = (0, 32, 64, 128, 192, 208, 224, 240, 256, 320)
CHUNKS = tuple((a, b - a) for a, b in zip(CUTS, CUTS[1:]))
EARLY = 4
TOGETHER = 8
MESH = pl.DeviceIdType.MESH
F32 = jnp.float32
BF16 = jnp.bfloat16


def pieces(value, count):
    out = []
    for _ in range(count - 1):
        head = value.astype(BF16)
        out.append(head)
        value = value - head.astype(F32)
    out.append(value.astype(BF16))
    return out


def mm(left, right):
    return jnp.dot(left, right, preferred_element_type=F32)


def mm_t(left, right):
    return lax.dot_general(left, right, (((1,), (1,)), ((), ())), preferred_element_type=F32)


def exact(left, right):
    a0, a1, a2 = pieces(left, 3)
    b0, b1, b2 = pieces(right, 3)
    a = jnp.concatenate([a0, a0, a1, a0, a2, a1], axis=1)
    b = jnp.concatenate([b0, b1, b0, b2, b0, b1], axis=0)
    return mm(a, b)


def exact_twice(left, right):
    a0, a1, a2 = pieces(left, 3)
    b0, b1, b2 = pieces(right, 3)
    low = lax.broadcasted_iota(jnp.int32, left.shape, 1) < PANEL
    a01 = jnp.where(low, left, left - a0.astype(F32)).astype(BF16)
    a12 = jnp.where(low, a1.astype(F32), a2.astype(F32)).astype(BF16)
    large = mm(jnp.concatenate([a0, a01], axis=1), jnp.concatenate([b0, b1, b2, b0], axis=0))
    return large + mm(a12, jnp.concatenate([b1, b0], axis=0))


def exact_t(left, right):
    a0, a1, a2 = pieces(left, 3)
    b0, b1, b2 = pieces(right, 3)
    a = jnp.concatenate([a0, a0, a1, a0, a2, a1], axis=1)
    b = jnp.concatenate([b0, b1, b0, b2, b0, b1], axis=1)
    return mm_t(a, b)


def identity(order):
    row = lax.broadcasted_iota(jnp.int32, (order, order), 0)
    return (row == lax.broadcasted_iota(jnp.int32, (order, order), 1)).astype(F32)


def inv_sqrt(correlation, between=()):
    eye = jnp.concatenate([identity(PANEL), identity(PANEL)], axis=1)
    twice = jnp.concatenate([correlation, correlation], axis=1)
    scale = jnp.sqrt(jnp.sum(correlation * correlation, keepdims=True))

    def turn(_, carry):
        root, inverse = carry
        factor = 0.5 * (3.0 * eye - exact_twice(inverse, root))
        return exact_twice(root, factor), exact_twice(factor, inverse)

    carry = (twice / scale, eye)
    parts = len(between) + 1
    for part in range(parts):
        turns = NS_ITERS * (part + 1) // parts - NS_ITERS * part // parts
        carry = lax.fori_loop(0, turns, turn, carry)
        if part < len(between):
            between[part]()
    return (carry[1] / jnp.sqrt(scale))[:, :PANEL]


def around(value, axis):
    return pltpu.roll(value, 1, axis) + pltpu.roll(value, value.shape[axis] - 1, axis)


def twelve_h(field, weighted, j):
    v, w = field[j], weighted[j]
    outer = field[j - 1] + field[j + 1]
    part = w - 2.0 * v - outer
    near = weighted[j - 1] + weighted[j + 1]
    return 24.0 * v + 6.0 * w - 2.0 * outer + near + around(part, 0) + around(part - around(v, 0), 1)


def filtered(v, pot):
    w = [a * b for a, b in zip(v, pot)]
    first = [None] + [twelve_h(v, w, j) * (1.0 / 18.0) - v[j] * (2.0 / 3.0) for j in range(1, 5)] + [None]
    w = [None] + [first[j] * pot[j] for j in range(1, 5)] + [None]
    return [twelve_h(first, w, j) * (1.0 / 9.0) - first[j] * (4.0 / 3.0) - v[j] for j in (2, 3)]


class Sum:
    def __init__(self, refs, rows, dom):
        self.loc, self.zin, self.part, self.xin, self.full, self.send, self.recv = refs
        self.n = rows // 4
        self.z = dom // 4
        self.x = lax.rem(dom, 4)
        self.zs = [lax.rem(self.z + k, 4) for k in (1, 2, 3)]
        self.xs = [lax.rem(self.x + k, 4) for k in (1, 2, 3)]

    def block(self, ref, z):
        return ref.at[pl.ds(pl.multiple_of(z * self.n, 8), self.n)]

    def copies(self, phase):
        out = []
        for k in range(3):
            if phase == 0:
                src, dst = self.block(self.loc, self.zs[k]), self.zin.at[k]
            elif phase == 1:
                src, dst = self.part, self.xin.at[k]
            else:
                src = dst = self.block(self.full, self.z)
            to = self.z * 4 + self.xs[k] if phase == 1 else self.zs[k] * 4 + self.x
            out.append(
                pltpu.make_async_remote_copy(
                    src_ref=src,
                    dst_ref=dst,
                    send_sem=self.send.at[phase, k],
                    recv_sem=self.recv.at[phase, k],
                    device_id={"dom": to},
                    device_id_type=MESH,
                )
            )
        return out

    def start(self):
        for copy in self.copies(0):
            copy.start()

    def over_z(self):
        for copy in self.copies(0):
            copy.wait_recv()
        mine = self.block(self.loc, self.z)
        self.part[...] = mine[...] + self.zin[0] + self.zin[1] + self.zin[2]
        for copy in self.copies(1):
            copy.start()

    def over_x(self):
        for copy in self.copies(1):
            copy.wait_recv()
        mine = self.block(self.full, self.z)
        mine[...] = self.part[...] + self.xin[0] + self.xin[1] + self.xin[2]
        for copy in self.copies(2):
            copy.start()

    def end(self):
        for copy in self.copies(2):
            copy.wait_recv()

    def sent(self):
        for phase in range(3):
            for copy in self.copies(phase):
                copy.wait_send()


def sum_scratch(rows):
    n = rows // 4
    return [
        pltpu.VMEM((rows, ALL), F32),
        pltpu.VMEM((3, n, ALL), F32),
        pltpu.VMEM((n, ALL), F32),
        pltpu.VMEM((3, n, ALL), F32),
        pltpu.VMEM((rows, ALL), F32),
        pltpu.SemaphoreType.DMA((3, 3)),
        pltpu.SemaphoreType.DMA((3, 3)),
    ]


BULK = 256


def body(orb, pot, y_out, p_out, d_out, own, left_in, right_in, pots, ym, pm, ph, plo, *rest):
    sums, sems = rest[:21], rest[21:]
    halo_s, halo_r, pot_s, pot_r, pan_s, pan_r, relay_s, local = sems
    dom, band = lax.axis_index("dom"), lax.axis_index("band")
    core, y = lax.rem(band, 2), band // 2
    right, left = lax.rem(dom + 1, DOM), lax.rem(dom + DOM - 1, DOM)
    gram = Sum(sums[:7], ALL, dom)
    bulk = Sum(sums[7:14], BULK, dom)
    last = Sum(sums[14:], ROWS - BULK, dom)

    barrier = pltpu.get_barrier_semaphore()
    peers = [{"dom": right}, {"dom": left}]
    peers += [{"dom": z * 4 + gram.x} for z in gram.zs] + [{"dom": gram.z * 4 + x} for x in gram.xs]
    peers += [{"band": lax.rem(band + k, BAND)} for k in range(1, BAND)]
    for peer in peers:
        pl.semaphore_signal(barrier, inc=1, device_id=peer, device_id_type=MESH)
    pl.semaphore_wait(barrier, len(peers))

    def remote(src, dst, send, recv, device):
        return pltpu.make_async_remote_copy(
            src_ref=src, dst_ref=dst, send_sem=send, recv_sem=recv, device_id=device, device_id_type=MESH
        )

    def halo(c):
        rows = pl.ds(*CHUNKS[c])
        return [
            remote(orb.at[rows], left_in.at[rows], halo_s.at[0, c], halo_r.at[0, c], {"dom": right}),
            remote(orb.at[rows], right_in.at[rows], halo_s.at[1, c], halo_r.at[1, c], {"dom": left}),
        ]

    def send_halo(c):
        for copy in halo(c):
            copy.start()

    def pot_halo():
        return [
            remote(pot, pots.at[0], pot_s.at[0], pot_r.at[0], {"dom": right}),
            remote(pot, pots.at[2], pot_s.at[1], pot_r.at[1], {"dom": left}),
        ]

    for copy in pot_halo():
        copy.start()
    for c in range(EARLY):
        send_halo(c)
    mine = [pltpu.make_async_copy(orb, own, local.at[0]), pltpu.make_async_copy(pot, pots.at[1], local.at[1])]
    for copy in mine:
        copy.start()
    for copy in mine:
        copy.wait()
    for copy in pot_halo():
        copy.wait_recv()

    flat = ym.reshape(16 * ROWS, 128)

    def run_filter(c):
        begin, count = CHUNKS[c]
        for copy in halo(c):
            copy.wait_recv()
        potential = [pots[j // 2, j % 2] for j in range(6)]

        def some(i, _):
            for step in range(TOGETHER):
                o = begin + TOGETHER * i + step
                v = [left_in[o, 0], left_in[o, 1], own[o, 0], own[o, 1], right_in[o, 0], right_in[o, 1]]
                for plane, value in enumerate(filtered(v, potential)):
                    flat[pl.ds(plane * 8 * ROWS + o, 8, stride=ROWS), :] = value
            return 0

        lax.fori_loop(0, count // TOGETHER, some, 0)

    def y_copy(c):
        rows = pl.ds(*CHUNKS[c])
        return pltpu.make_async_copy(ym.at[:, rows], y_out.at[:, rows], local.at[2 + c])

    def panel_rows(p, half):
        return pm.at[:, pl.ds(p * PANEL + half * 32, 32)]

    def owner_copies(p, half):
        rows = ym.at[:, pl.ds(half * 32, 32)]
        targets = [p ^ 1, (p + 2) % BAND, (p + 4) % BAND, (p + 6) % BAND]
        return [
            remote(rows, panel_rows(p, half), pan_s.at[half, k], pan_r.at[p, half], {"band": t})
            for k, t in enumerate(targets)
        ]

    def relay_copy(p, half):
        ref = panel_rows(p, half)
        return remote(ref, ref, relay_s.at[p, half], pan_r.at[p, half], {"band": band + 1 - 2 * core})

    def relays(p):
        return (core == p % 2) & (y != p // 2)

    def send_panel(half):
        for p in range(PANELS):

            @pl.when(band == p)
            def _():
                for copy in owner_copies(p, half):
                    copy.start()
                begin, count = CHUNKS[half]
                pm[:, p * PANEL + begin : p * PANEL + begin + count] = ym[:, begin : begin + count]

    def take_panel(half):
        for p in range(PANELS):

            @pl.when(band != p)
            def _():
                relay_copy(p, half).wait_recv()

            @pl.when(relays(p))
            def _():
                relay_copy(p, half).start()

    def inner(begin, count, total, at):
        def some(k, acc):
            a0, a1 = pieces(ym[k, begin : begin + count], 2)
            b0, b1 = ph[k], plo[k]
            both = mm_t(jnp.concatenate([a0, a1], axis=1), jnp.concatenate([b0, b0], axis=1))
            return acc + (both + mm_t(a0, b1))

        total.loc[at : at + count] = lax.fori_loop(0, 16, some, jnp.zeros((count, ALL), F32), unroll=4)

    run_filter(0)
    send_panel(0)
    run_filter(1)
    send_panel(1)
    take_panel(0)
    run_filter(2)
    y_copy(2).start()
    take_panel(1)

    p_copy = pltpu.make_async_copy(pm, p_out, local.at[2 + len(CHUNKS)])
    p_copy.start()

    def gram_step(k, acc):
        a0, a1 = pieces(pm[k], 2)
        ph[k] = a0
        plo[k] = a1
        return acc + (mm_t(a0, a0) + (mm_t(a0, a1) + mm_t(a1, a0)))

    gram.loc[...] = lax.fori_loop(0, 16, gram_step, jnp.zeros((ALL, ALL), F32), unroll=4)
    gram.start()
    send_halo(4)
    inner(0, 128, bulk, 0)
    gram.over_z()
    send_halo(5)
    for half in range(2):
        for p in range(PANELS):

            @pl.when(band == p)
            def _():
                for copy in owner_copies(p, half):
                    copy.wait_send()
                begin, count = CHUNKS[half]
                ym[:, begin : begin + count] = jnp.zeros((16, count, 128), F32)

        y_copy(half).start()
    run_filter(3)
    y_copy(3).start()
    send_halo(6)
    gram.over_x()
    send_halo(7)
    gram.end()
    send_halo(8)

    g = gram.full[...]
    eye = identity(PANEL)
    none = jnp.zeros((PANEL, PANEL), F32)
    t0 = jnp.concatenate([inv_sqrt(g[:PANEL, :PANEL]), none, none], axis=1)
    t0g = exact(t0, g)
    a = jnp.concatenate([jnp.concatenate([none, eye, none], axis=1), jnp.concatenate([none, none, eye], axis=1)], axis=0)
    a = a - exact(exact_t(g[PANEL:], t0), t0)
    ag = exact(a, g)
    s1 = exact_t(ag[:PANEL], a[:PANEL])
    for c in (4, 5, 6, 7):
        run_filter(c)
        y_copy(c).start()
    inner(128, 128, bulk, 128)
    bulk.start()
    t1 = exact(inv_sqrt(s1), a[:PANEL])
    t1g = exact(t1, g)
    bulk.over_z()
    a = a[PANEL:] - exact(exact_t(ag[PANEL:], t1), t1)
    s2 = exact_t(exact(a, g), a)
    for c in (8,):
        run_filter(c)
        y_copy(c).start()
    inner(BULK, ROWS - BULK, last, 0)
    last.start()
    t2 = exact(inv_sqrt(s2, (bulk.over_x, last.over_z)), a)
    bulk.end()
    last.over_x()
    t2g = exact(t2, g)
    r0 = t0
    r1 = t1 - exact(exact_t(t1g, t0), r0)
    r2 = t2 - exact(exact_t(t2g, t0), r0) - exact(exact_t(t2g, t1), r1)
    t = jnp.concatenate([t0, t1, t2], axis=0)
    r = jnp.concatenate([r0, r1, r2], axis=0)
    d_out[:BULK] = exact(exact_t(bulk.full[...], r), t)
    for p, rows in enumerate((t0, t1, t2)):

        @pl.when(band == p)
        def _():
            d_out[:PANEL] = -rows

    last.end()
    d_out[BULK:] = exact(exact_t(last.full[...], r), t)

    for c in range(len(CHUNKS)):
        for copy in halo(c):
            copy.wait_send()
        y_copy(c).wait()
    for copy in pot_halo():
        copy.wait_send()
    for half in range(2):
        for p in range(PANELS):

            @pl.when(relays(p))
            def _():
                relay_copy(p, half).wait_send()

    p_copy.wait()
    for total in (gram, bulk, last):
        total.sent()


def project(orb, pot):
    scratch = [pltpu.VMEM((ROWS, 2, 8, 128), F32)] * 3 + [
        pltpu.VMEM((3, 2, 8, 128), F32),
        pltpu.VMEM((16, ROWS, 128), F32),
        pltpu.VMEM((16, ALL, 128), F32),
        pltpu.VMEM((16, ALL, 128), BF16),
        pltpu.VMEM((16, ALL, 128), BF16),
    ]
    scratch += sum_scratch(ALL) + sum_scratch(BULK) + sum_scratch(ROWS - BULK)
    scratch += [
        pltpu.SemaphoreType.DMA((2, len(CHUNKS))),
        pltpu.SemaphoreType.DMA((2, len(CHUNKS))),
        pltpu.SemaphoreType.DMA((2,)),
        pltpu.SemaphoreType.DMA((2,)),
        pltpu.SemaphoreType.DMA((2, 4)),
        pltpu.SemaphoreType.DMA((PANELS, 2)),
        pltpu.SemaphoreType.DMA((PANELS, 2)),
        pltpu.SemaphoreType.DMA((3 + len(CHUNKS),)),
    ]
    anywhere = pl.BlockSpec(memory_space=pltpu.HBM)
    return pl.pallas_call(
        body,
        out_shape=(
            jax.ShapeDtypeStruct((16, ROWS, 128), F32),
            jax.ShapeDtypeStruct((16, ALL, 128), F32),
            jax.ShapeDtypeStruct((ROWS, ALL), F32),
        ),
        in_specs=[anywhere, anywhere],
        out_specs=(anywhere, anywhere, pl.BlockSpec(memory_space=pltpu.VMEM)),
        scratch_shapes=scratch,
        compiler_params=pltpu.CompilerParams(collective_id=0, has_side_effects=True, vmem_limit_bytes=40 << 20),
        name="filter_and_project",
    )(orb, pot)


STEP = 160


def update_body(y, p, d, out, ph, plo):
    @pl.when(pl.program_id(0) == 0)
    def _():
        def cast(k, _):
            ph[k], plo[k] = pieces(p[k], 2)
            return 0

        lax.fori_loop(0, 16, cast, 0)

    d0, d1 = pieces(d[...], 2)
    flat = out.reshape(STEP * 16, 128)

    def some(k, _):
        rows = y[k] - (mm(d0, ph[k]) + (mm(d0, plo[k]) + mm(d1, ph[k])))
        for i in range(STEP // 8):
            flat[pl.ds(i * 128 + k, 8, stride=16), :] = rows[i * 8 : i * 8 + 8]
        return 0

    lax.fori_loop(0, 16, some, 0, unroll=4)


def update(y, p, d):
    return pl.pallas_call(
        update_body,
        grid=(ROWS // STEP,),
        out_shape=jax.ShapeDtypeStruct((ROWS, 2, 8, 128), F32),
        in_specs=[
            pl.BlockSpec((16, STEP, 128), lambda i: (0, i, 0)),
            pl.BlockSpec((16, ALL, 128), lambda i: (0, 0, 0), pipeline_mode=pl.Buffered(1)),
            pl.BlockSpec((STEP, ALL), lambda i: (i, 0)),
        ],
        out_specs=pl.BlockSpec((STEP, 2, 8, 128), lambda i: (i, 0, 0, 0)),
        scratch_shapes=[pltpu.VMEM((16, ALL, 128), BF16), pltpu.VMEM((16, ALL, 128), BF16)],
        compiler_params=pltpu.CompilerParams(vmem_limit_bytes=24 << 20),
        name="apply_update",
    )(y, p, d)


def per_device(orbitals, potential):
    return update(*project(orbitals, potential))


def solution(mesh):
    spec = P("band", "dom", None, None)
    return jax.shard_map(
        per_device, mesh=mesh, in_specs=(spec, P("dom", None, None)), out_specs=spec, check_vma=False
    )
```

```python
import jax
import jax.numpy as jnp
from jax import lax
from jax.experimental import pallas as pl
from jax.experimental.pallas import tpu as pltpu
from jax.sharding import PartitionSpec as P

PANEL = 64
PANELS = 3
NS_ITERS = 16
ROWS = 320
DOM = 16
BAND = 8
ALL = PANEL * PANELS
CUTS = (0, 32, 64, 128, 192, 208, 224, 240, 256, 320)
CHUNKS = tuple((a, b - a) for a, b in zip(CUTS, CUTS[1:]))
EARLY = 4
TOGETHER = 8
MESH = pl.DeviceIdType.MESH
F32 = jnp.float32
BF16 = jnp.bfloat16


def pieces(value, count):
    out = []
    for _ in range(count - 1):
        head = value.astype(BF16)
        out.append(head)
        value = value - head.astype(F32)
    out.append(value.astype(BF16))
    return out


def mm(left, right):
    return jnp.dot(left, right, preferred_element_type=F32)


def mm_t(left, right):
    return lax.dot_general(left, right, (((1,), (1,)), ((), ())), preferred_element_type=F32)


def exact(left, right):
    a0, a1, a2 = pieces(left, 3)
    b0, b1, b2 = pieces(right, 3)
    a = jnp.concatenate([a0, a0, a1, a0, a2, a1], axis=1)
    b = jnp.concatenate([b0, b1, b0, b2, b0, b1], axis=0)
    return mm(a, b)


def exact_twice(left, right):
    a0, a1, a2 = pieces(left, 3)
    b0, b1, b2 = pieces(right, 3)
    low = lax.broadcasted_iota(jnp.int32, left.shape, 1) < PANEL
    a01 = jnp.where(low, left, left - a0.astype(F32)).astype(BF16)
    a12 = jnp.where(low, a1.astype(F32), a2.astype(F32)).astype(BF16)
    large = mm(jnp.concatenate([a0, a01], axis=1), jnp.concatenate([b0, b1, b2, b0], axis=0))
    return large + mm(a12, jnp.concatenate([b1, b0], axis=0))


def exact_t(left, right):
    a0, a1, a2 = pieces(left, 3)
    b0, b1, b2 = pieces(right, 3)
    a = jnp.concatenate([a0, a0, a1, a0, a2, a1], axis=1)
    b = jnp.concatenate([b0, b1, b0, b2, b0, b1], axis=1)
    return mm_t(a, b)


def identity(order):
    row = lax.broadcasted_iota(jnp.int32, (order, order), 0)
    return (row == lax.broadcasted_iota(jnp.int32, (order, order), 1)).astype(F32)


def inv_sqrt(correlation, between=()):
    eye = jnp.concatenate([identity(PANEL), identity(PANEL)], axis=1)
    twice = jnp.concatenate([correlation, correlation], axis=1)
    scale = jnp.sqrt(jnp.sum(correlation * correlation, keepdims=True))

    def turn(_, carry):
        root, inverse = carry
        factor = 0.5 * (3.0 * eye - exact_twice(inverse, root))
        return exact_twice(root, factor), exact_twice(factor, inverse)

    carry = (twice / scale, eye)
    parts = len(between) + 1
    for part in range(parts):
        turns = NS_ITERS * (part + 1) // parts - NS_ITERS * part // parts
        carry = lax.fori_loop(0, turns, turn, carry)
        if part < len(between):
            between[part]()
    return (carry[1] / jnp.sqrt(scale))[:, :PANEL]


def around(value, axis):
    return pltpu.roll(value, 1, axis) + pltpu.roll(value, value.shape[axis] - 1, axis)


def twelve_h(field, weighted, j):
    v, w = field[j], weighted[j]
    outer = field[j - 1] + field[j + 1]
    part = w - 2.0 * v - outer
    near = weighted[j - 1] + weighted[j + 1]
    return 24.0 * v + 6.0 * w - 2.0 * outer + near + around(part, 0) + around(part - around(v, 0), 1)


def filtered(v, pot):
    w = [a * b for a, b in zip(v, pot)]
    first = [None] + [twelve_h(v, w, j) * (1.0 / 18.0) - v[j] * (2.0 / 3.0) for j in range(1, 5)] + [None]
    w = [None] + [first[j] * pot[j] for j in range(1, 5)] + [None]
    return [twelve_h(first, w, j) * (1.0 / 9.0) - first[j] * (4.0 / 3.0) - v[j] for j in (2, 3)]


class Sum:
    def __init__(self, refs, rows, dom):
        self.loc, self.zin, self.part, self.xin, self.full, self.send, self.recv = refs
        self.n = rows // 4
        self.z = dom // 4
        self.x = lax.rem(dom, 4)
        self.zs = [lax.rem(self.z + k, 4) for k in (1, 2, 3)]
        self.xs = [lax.rem(self.x + k, 4) for k in (1, 2, 3)]

    def block(self, ref, z):
        return ref.at[pl.ds(pl.multiple_of(z * self.n, 8), self.n)]

    def copies(self, phase):
        out = []
        for k in range(3):
            if phase == 0:
                src, dst = self.block(self.loc, self.zs[k]), self.zin.at[k]
            elif phase == 1:
                src, dst = self.part, self.xin.at[k]
            else:
                src = dst = self.block(self.full, self.z)
            to = self.z * 4 + self.xs[k] if phase == 1 else self.zs[k] * 4 + self.x
            out.append(
                pltpu.make_async_remote_copy(
                    src_ref=src,
                    dst_ref=dst,
                    send_sem=self.send.at[phase, k],
                    recv_sem=self.recv.at[phase, k],
                    device_id={"dom": to},
                    device_id_type=MESH,
                )
            )
        return out

    def start(self):
        for copy in self.copies(0):
            copy.start()

    def over_z(self):
        for copy in self.copies(0):
            copy.wait_recv()
        mine = self.block(self.loc, self.z)
        self.part[...] = mine[...] + self.zin[0] + self.zin[1] + self.zin[2]
        for copy in self.copies(1):
            copy.start()

    def over_x(self):
        for copy in self.copies(1):
            copy.wait_recv()
        mine = self.block(self.full, self.z)
        mine[...] = self.part[...] + self.xin[0] + self.xin[1] + self.xin[2]
        for copy in self.copies(2):
            copy.start()

    def end(self):
        for copy in self.copies(2):
            copy.wait_recv()

    def sent(self):
        for phase in range(3):
            for copy in self.copies(phase):
                copy.wait_send()


def sum_scratch(rows):
    n = rows // 4
    return [
        pltpu.VMEM((rows, ALL), F32),
        pltpu.VMEM((3, n, ALL), F32),
        pltpu.VMEM((n, ALL), F32),
        pltpu.VMEM((3, n, ALL), F32),
        pltpu.VMEM((rows, ALL), F32),
        pltpu.SemaphoreType.DMA((3, 3)),
        pltpu.SemaphoreType.DMA((3, 3)),
    ]


BULK = 256


def body(orb, pot, y_out, p_out, d_out, own, left_in, right_in, pots, ym, pm, ph, plo, *rest):
    sums, sems = rest[:21], rest[21:]
    halo_s, halo_r, pot_s, pot_r, pan_s, pan_r, relay_s, local = sems
    dom, band = lax.axis_index("dom"), lax.axis_index("band")
    core, y = lax.rem(band, 2), band // 2
    right, left = lax.rem(dom + 1, DOM), lax.rem(dom + DOM - 1, DOM)
    gram = Sum(sums[:7], ALL, dom)
    bulk = Sum(sums[7:14], BULK, dom)
    last = Sum(sums[14:], ROWS - BULK, dom)

    barrier = pltpu.get_barrier_semaphore()
    peers = [{"dom": right}, {"dom": left}]
    peers += [{"dom": z * 4 + gram.x} for z in gram.zs] + [{"dom": gram.z * 4 + x} for x in gram.xs]
    peers += [{"band": lax.rem(band + k, BAND)} for k in range(1, BAND)]
    for peer in peers:
        pl.semaphore_signal(barrier, inc=1, device_id=peer, device_id_type=MESH)
    pl.semaphore_wait(barrier, len(peers))

    def remote(src, dst, send, recv, device):
        return pltpu.make_async_remote_copy(
            src_ref=src, dst_ref=dst, send_sem=send, recv_sem=recv, device_id=device, device_id_type=MESH
        )

    def halo(c):
        rows = pl.ds(*CHUNKS[c])
        return [
            remote(orb.at[rows], left_in.at[rows], halo_s.at[0, c], halo_r.at[0, c], {"dom": right}),
            remote(orb.at[rows], right_in.at[rows], halo_s.at[1, c], halo_r.at[1, c], {"dom": left}),
        ]

    def send_halo(c):
        for copy in halo(c):
            copy.start()

    def send_inside(c):
        for copy, edge in zip(halo(c), (3, 0)):
            pl.when(gram.x != edge)(copy.start)

    def send_around(c):
        for copy, edge in zip(halo(c), (3, 0)):
            pl.when(gram.x == edge)(copy.start)

    def pot_halo():
        return [
            remote(pot, pots.at[0], pot_s.at[0], pot_r.at[0], {"dom": right}),
            remote(pot, pots.at[2], pot_s.at[1], pot_r.at[1], {"dom": left}),
        ]

    for copy in pot_halo():
        copy.start()
    for c in range(EARLY):
        send_halo(c)
    mine = [pltpu.make_async_copy(orb, own, local.at[0]), pltpu.make_async_copy(pot, pots.at[1], local.at[1])]
    for copy in mine:
        copy.start()
    for copy in mine:
        copy.wait()
    for copy in pot_halo():
        copy.wait_recv()

    flat = ym.reshape(16 * ROWS, 128)

    def run_filter(c):
        begin, count = CHUNKS[c]
        for copy in halo(c):
            copy.wait_recv()
        potential = [pots[j // 2, j % 2] for j in range(6)]

        def some(i, _):
            for step in range(TOGETHER):
                o = begin + TOGETHER * i + step
                v = [left_in[o, 0], left_in[o, 1], own[o, 0], own[o, 1], right_in[o, 0], right_in[o, 1]]
                for plane, value in enumerate(filtered(v, potential)):
                    flat[pl.ds(plane * 8 * ROWS + o, 8, stride=ROWS), :] = value
            return 0

        lax.fori_loop(0, count // TOGETHER, some, 0)

    def y_copy(c):
        rows = pl.ds(*CHUNKS[c])
        return pltpu.make_async_copy(ym.at[:, rows], y_out.at[:, rows], local.at[2 + c])

    def panel_rows(p, half):
        return pm.at[:, pl.ds(p * PANEL + half * 32, 32)]

    def owner_copies(p, half):
        rows = ym.at[:, pl.ds(half * 32, 32)]
        targets = [p ^ 1, (p + 2) % BAND, (p + 4) % BAND, (p + 6) % BAND]
        return [
            remote(rows, panel_rows(p, half), pan_s.at[half, k], pan_r.at[p, half], {"band": t})
            for k, t in enumerate(targets)
        ]

    def relay_copy(p, half):
        ref = panel_rows(p, half)
        return remote(ref, ref, relay_s.at[p, half], pan_r.at[p, half], {"band": band + 1 - 2 * core})

    def relays(p):
        return (core == p % 2) & (y != p // 2)

    def send_panel(half):
        for p in range(PANELS):

            @pl.when(band == p)
            def _():
                for copy in owner_copies(p, half):
                    copy.start()
                begin, count = CHUNKS[half]
                pm[:, p * PANEL + begin : p * PANEL + begin + count] = ym[:, begin : begin + count]

    def take_panel(half):
        for p in range(PANELS):

            @pl.when(band != p)
            def _():
                relay_copy(p, half).wait_recv()

            @pl.when(relays(p))
            def _():
                relay_copy(p, half).start()

    def inner(begin, count, total, at):
        def some(k, acc):
            a0, a1 = pieces(ym[k, begin : begin + count], 2)
            b0, b1 = ph[k], plo[k]
            both = mm_t(jnp.concatenate([a0, a1], axis=1), jnp.concatenate([b0, b0], axis=1))
            return acc + (both + mm_t(a0, b1))

        total.loc[at : at + count] = lax.fori_loop(0, 16, some, jnp.zeros((count, ALL), F32), unroll=4)

    run_filter(0)
    send_panel(0)
    run_filter(1)
    send_panel(1)
    take_panel(0)
    run_filter(2)
    y_copy(2).start()
    take_panel(1)

    p_copy = pltpu.make_async_copy(pm, p_out, local.at[2 + len(CHUNKS)])
    p_copy.start()

    def gram_step(k, acc):
        a0, a1 = pieces(pm[k], 2)
        ph[k] = a0
        plo[k] = a1
        return acc + (mm_t(a0, a0) + (mm_t(a0, a1) + mm_t(a1, a0)))

    gram.loc[...] = lax.fori_loop(0, 16, gram_step, jnp.zeros((ALL, ALL), F32), unroll=4)
    gram.start()
    send_halo(4)
    inner(0, 128, bulk, 0)
    gram.over_z()
    send_inside(5)
    for half in range(2):
        for p in range(PANELS):

            @pl.when(band == p)
            def _():
                for copy in owner_copies(p, half):
                    copy.wait_send()
                begin, count = CHUNKS[half]
                ym[:, begin : begin + count] = jnp.zeros((16, count, 128), F32)

        y_copy(half).start()
    run_filter(3)
    y_copy(3).start()
    send_inside(6)
    gram.over_x()
    send_inside(7)
    send_inside(8)
    gram.end()
    send_around(5)
    send_around(6)
    send_around(7)
    send_around(8)

    g = gram.full[...]
    eye = identity(PANEL)
    none = jnp.zeros((PANEL, PANEL), F32)
    t0 = jnp.concatenate([inv_sqrt(g[:PANEL, :PANEL]), none, none], axis=1)
    a = jnp.concatenate([jnp.concatenate([none, eye, none], axis=1), jnp.concatenate([none, none, eye], axis=1)], axis=0)
    a = a - exact(exact_t(g[PANEL:], t0), t0)
    ag = exact(a, g)
    s1 = exact_t(ag[:PANEL], a[:PANEL])
    for c in (4, 5, 6, 7):
        run_filter(c)
        y_copy(c).start()
    inner(128, 128, bulk, 128)
    bulk.start()
    root1 = inv_sqrt(s1)
    t1 = exact(root1, a[:PANEL])
    r1 = t1 - exact(exact_t(exact(root1, ag[:PANEL]), t0), t0)
    t01 = jnp.concatenate([t0, t1], axis=0)
    r01 = jnp.concatenate([t0, r1], axis=0)
    bulk.over_z()
    a2 = a[PANEL:] - exact(exact_t(ag[PANEL:], t1), t1)
    a2g = exact(a2, g)
    s2 = exact_t(a2g, a2)
    for c in (8,):
        run_filter(c)
        y_copy(c).start()
    inner(BULK, ROWS - BULK, last, 0)
    last.start()
    root2 = inv_sqrt(s2, (bulk.over_x, last.over_z, last.over_x))
    t2 = exact(root2, a2)
    before = exact_t(exact(root2, a2g), t01)
    bulk.end()
    t = jnp.concatenate([t01, t2], axis=0)
    r = jnp.concatenate([r01, t2 - exact(before, r01)], axis=0)
    d_out[:BULK] = exact(exact_t(bulk.full[...], r), t)
    for p, rows in enumerate((t0, t1, t2)):

        @pl.when(band == p)
        def _():
            d_out[:PANEL] = -rows

    last.end()
    d_out[BULK:] = exact(exact_t(last.full[...], r), t)

    for c in range(len(CHUNKS)):
        for copy in halo(c):
            copy.wait_send()
        y_copy(c).wait()
    for copy in pot_halo():
        copy.wait_send()
    for half in range(2):
        for p in range(PANELS):

            @pl.when(relays(p))
            def _():
                relay_copy(p, half).wait_send()

    p_copy.wait()
    for total in (gram, bulk, last):
        total.sent()


def project(orb, pot):
    scratch = [pltpu.VMEM((ROWS, 2, 8, 128), F32)] * 3 + [
        pltpu.VMEM((3, 2, 8, 128), F32),
        pltpu.VMEM((16, ROWS, 128), F32),
        pltpu.VMEM((16, ALL, 128), F32),
        pltpu.VMEM((16, ALL, 128), BF16),
        pltpu.VMEM((16, ALL, 128), BF16),
    ]
    scratch += sum_scratch(ALL) + sum_scratch(BULK) + sum_scratch(ROWS - BULK)
    scratch += [
        pltpu.SemaphoreType.DMA((2, len(CHUNKS))),
        pltpu.SemaphoreType.DMA((2, len(CHUNKS))),
        pltpu.SemaphoreType.DMA((2,)),
        pltpu.SemaphoreType.DMA((2,)),
        pltpu.SemaphoreType.DMA((2, 4)),
        pltpu.SemaphoreType.DMA((PANELS, 2)),
        pltpu.SemaphoreType.DMA((PANELS, 2)),
        pltpu.SemaphoreType.DMA((3 + len(CHUNKS),)),
    ]
    anywhere = pl.BlockSpec(memory_space=pltpu.HBM)
    return pl.pallas_call(
        body,
        out_shape=(
            jax.ShapeDtypeStruct((16, ROWS, 128), F32),
            jax.ShapeDtypeStruct((16, ALL, 128), F32),
            jax.ShapeDtypeStruct((ROWS, ALL), F32),
        ),
        in_specs=[anywhere, anywhere],
        out_specs=(anywhere, anywhere, pl.BlockSpec(memory_space=pltpu.VMEM)),
        scratch_shapes=scratch,
        compiler_params=pltpu.CompilerParams(collective_id=0, has_side_effects=True, vmem_limit_bytes=40 << 20),
        name="filter_and_project",
    )(orb, pot)


STEP = 160


def update_body(y, p, d, out, ph, plo):
    @pl.when(pl.program_id(0) == 0)
    def _():
        def cast(k, _):
            ph[k], plo[k] = pieces(p[k], 2)
            return 0

        lax.fori_loop(0, 16, cast, 0)

    d0, d1 = pieces(d[...], 2)
    flat = out.reshape(STEP * 16, 128)

    def some(k, _):
        rows = y[k] - (mm(d0, ph[k]) + (mm(d0, plo[k]) + mm(d1, ph[k])))
        for i in range(STEP // 8):
            flat[pl.ds(i * 128 + k, 8, stride=16), :] = rows[i * 8 : i * 8 + 8]
        return 0

    lax.fori_loop(0, 16, some, 0, unroll=8)


def update(y, p, d):
    return pl.pallas_call(
        update_body,
        grid=(ROWS // STEP,),
        out_shape=jax.ShapeDtypeStruct((ROWS, 2, 8, 128), F32),
        in_specs=[
            pl.BlockSpec((16, STEP, 128), lambda i: (0, i, 0)),
            pl.BlockSpec((16, ALL, 128), lambda i: (0, 0, 0), pipeline_mode=pl.Buffered(1)),
            pl.BlockSpec((STEP, ALL), lambda i: (i, 0)),
        ],
        out_specs=pl.BlockSpec((STEP, 2, 8, 128), lambda i: (i, 0, 0, 0)),
        scratch_shapes=[pltpu.VMEM((16, ALL, 128), BF16), pltpu.VMEM((16, ALL, 128), BF16)],
        compiler_params=pltpu.CompilerParams(vmem_limit_bytes=24 << 20),
        name="apply_update",
    )(y, p, d)


def per_device(orbitals, potential):
    return update(*project(orbitals, potential))


def solution(mesh):
    spec = P("band", "dom", None, None)
    return jax.shard_map(
        per_device, mesh=mesh, in_specs=(spec, P("dom", None, None)), out_specs=spec, check_vma=False
    )
```

```python
import jax
import jax.numpy as jnp
from jax import lax
from jax.experimental import pallas as pl
from jax.experimental.pallas import tpu as pltpu
from jax.sharding import PartitionSpec as P

PANEL = 64
PANELS = 3
NS_ITERS = 16
ROWS = 320
DOM = 16
BAND = 8
ALL = PANEL * PANELS
CUTS = (0, 32, 64, 128, 192, 208, 224, 240, 256, 320)
CHUNKS = tuple((a, b - a) for a, b in zip(CUTS, CUTS[1:]))
EARLY = 4
TOGETHER = 8
MESH = pl.DeviceIdType.MESH
F32 = jnp.float32
BF16 = jnp.bfloat16


def pieces(value, count):
    out = []
    for _ in range(count - 1):
        head = value.astype(BF16)
        out.append(head)
        value = value - head.astype(F32)
    out.append(value.astype(BF16))
    return out


def mm(left, right):
    return jnp.dot(left, right, preferred_element_type=F32)


def mm_t(left, right):
    return lax.dot_general(left, right, (((1,), (1,)), ((), ())), preferred_element_type=F32)


def exact(left, right):
    a0, a1, a2 = pieces(left, 3)
    b0, b1, b2 = pieces(right, 3)
    a = jnp.concatenate([a0, a0, a1, a0, a2, a1], axis=1)
    b = jnp.concatenate([b0, b1, b0, b2, b0, b1], axis=0)
    return mm(a, b)


def exact_twice(left, right):
    a0, a1, a2 = pieces(left, 3)
    b0, b1, b2 = pieces(right, 3)
    low = lax.broadcasted_iota(jnp.int32, left.shape, 1) < PANEL
    a01 = jnp.where(low, left, left - a0.astype(F32)).astype(BF16)
    a12 = jnp.where(low, a1.astype(F32), a2.astype(F32)).astype(BF16)
    large = mm(jnp.concatenate([a0, a01], axis=1), jnp.concatenate([b0, b1, b2, b0], axis=0))
    return large + mm(a12, jnp.concatenate([b1, b0], axis=0))


def exact_t(left, right):
    a0, a1, a2 = pieces(left, 3)
    b0, b1, b2 = pieces(right, 3)
    a = jnp.concatenate([a0, a0, a1, a0, a2, a1], axis=1)
    b = jnp.concatenate([b0, b1, b0, b2, b0, b1], axis=1)
    return mm_t(a, b)


def identity(order):
    row = lax.broadcasted_iota(jnp.int32, (order, order), 0)
    return (row == lax.broadcasted_iota(jnp.int32, (order, order), 1)).astype(F32)


def inv_sqrt(correlation, between=()):
    eye = jnp.concatenate([identity(PANEL), identity(PANEL)], axis=1)
    twice = jnp.concatenate([correlation, correlation], axis=1)
    scale = jnp.sqrt(jnp.sum(correlation * correlation, keepdims=True))

    def turn(_, carry):
        root, inverse = carry
        factor = 0.5 * (3.0 * eye - exact_twice(inverse, root))
        return exact_twice(root, factor), exact_twice(factor, inverse)

    carry = (twice / scale, eye)
    parts = len(between) + 1
    for part in range(parts):
        turns = NS_ITERS * (part + 1) // parts - NS_ITERS * part // parts
        carry = lax.fori_loop(0, turns, turn, carry)
        if part < len(between):
            between[part]()
    return (carry[1] / jnp.sqrt(scale))[:, :PANEL]


def around(value, axis):
    return pltpu.roll(value, 1, axis) + pltpu.roll(value, value.shape[axis] - 1, axis)


def twelve_h(field, weighted, j):
    v, w = field[j], weighted[j]
    outer = field[j - 1] + field[j + 1]
    part = w - 2.0 * v - outer
    near = weighted[j - 1] + weighted[j + 1]
    return 24.0 * v + 6.0 * w - 2.0 * outer + near + around(part, 0) + around(part - around(v, 0), 1)


def filtered(v, pot):
    w = [a * b for a, b in zip(v, pot)]
    first = [None] + [twelve_h(v, w, j) * (1.0 / 18.0) - v[j] * (2.0 / 3.0) for j in range(1, 5)] + [None]
    w = [None] + [first[j] * pot[j] for j in range(1, 5)] + [None]
    return [twelve_h(first, w, j) * (1.0 / 9.0) - first[j] * (4.0 / 3.0) - v[j] for j in (2, 3)]


class Sum:
    def __init__(self, refs, rows, dom):
        self.loc, self.zin, self.part, self.xin, self.full, self.send, self.recv = refs
        self.n = rows // 4
        self.z = dom // 4
        self.x = lax.rem(dom, 4)
        self.zs = [lax.rem(self.z + k, 4) for k in (1, 2, 3)]
        self.xs = [lax.rem(self.x + k, 4) for k in (1, 2, 3)]

    def block(self, ref, z):
        return ref.at[pl.ds(pl.multiple_of(z * self.n, 8), self.n)]

    def copies(self, phase):
        out = []
        for k in range(3):
            if phase == 0:
                src, dst = self.block(self.loc, self.zs[k]), self.zin.at[k]
            elif phase == 1:
                src, dst = self.part, self.xin.at[k]
            else:
                src = dst = self.block(self.full, self.z)
            to = self.z * 4 + self.xs[k] if phase == 1 else self.zs[k] * 4 + self.x
            out.append(
                pltpu.make_async_remote_copy(
                    src_ref=src,
                    dst_ref=dst,
                    send_sem=self.send.at[phase, k],
                    recv_sem=self.recv.at[phase, k],
                    device_id={"dom": to},
                    device_id_type=MESH,
                )
            )
        return out

    def start(self):
        for copy in self.copies(0):
            copy.start()

    def over_z(self):
        for copy in self.copies(0):
            copy.wait_recv()
        mine = self.block(self.loc, self.z)
        self.part[...] = mine[...] + self.zin[0] + self.zin[1] + self.zin[2]
        for copy in self.copies(1):
            copy.start()

    def over_x(self):
        for copy in self.copies(1):
            copy.wait_recv()
        mine = self.block(self.full, self.z)
        mine[...] = self.part[...] + self.xin[0] + self.xin[1] + self.xin[2]
        for copy in self.copies(2):
            copy.start()

    def end(self):
        for copy in self.copies(2):
            copy.wait_recv()

    def sent(self):
        for phase in range(3):
            for copy in self.copies(phase):
                copy.wait_send()


def sum_scratch(rows):
    n = rows // 4
    return [
        pltpu.VMEM((rows, ALL), F32),
        pltpu.VMEM((3, n, ALL), F32),
        pltpu.VMEM((n, ALL), F32),
        pltpu.VMEM((3, n, ALL), F32),
        pltpu.VMEM((rows, ALL), F32),
        pltpu.SemaphoreType.DMA((3, 3)),
        pltpu.SemaphoreType.DMA((3, 3)),
    ]


BULK = 256


def body(orb, pot, y_out, p_out, d_out, own, left_in, right_in, pots, ym, pm, ph, plo, *rest):
    sums, sems = rest[:21], rest[21:]
    halo_s, halo_r, pot_s, pot_r, pan_s, pan_r, relay_s, local = sems
    dom, band = lax.axis_index("dom"), lax.axis_index("band")
    core, y = lax.rem(band, 2), band // 2
    right, left = lax.rem(dom + 1, DOM), lax.rem(dom + DOM - 1, DOM)
    gram = Sum(sums[:7], ALL, dom)
    bulk = Sum(sums[7:14], BULK, dom)
    last = Sum(sums[14:], ROWS - BULK, dom)

    barrier = pltpu.get_barrier_semaphore()
    peers = [{"dom": right}, {"dom": left}]
    peers += [{"dom": z * 4 + gram.x} for z in gram.zs] + [{"dom": gram.z * 4 + x} for x in gram.xs]
    peers += [{"band": lax.rem(band + k, BAND)} for k in range(1, BAND)]
    for peer in peers:
        pl.semaphore_signal(barrier, inc=1, device_id=peer, device_id_type=MESH)
    pl.semaphore_wait(barrier, len(peers))

    def remote(src, dst, send, recv, device):
        return pltpu.make_async_remote_copy(
            src_ref=src, dst_ref=dst, send_sem=send, recv_sem=recv, device_id=device, device_id_type=MESH
        )

    def halo(c):
        rows = pl.ds(*CHUNKS[c])
        return [
            remote(orb.at[rows], left_in.at[rows], halo_s.at[0, c], halo_r.at[0, c], {"dom": right}),
            remote(orb.at[rows], right_in.at[rows], halo_s.at[1, c], halo_r.at[1, c], {"dom": left}),
        ]

    def send_halo(c):
        for copy in halo(c):
            copy.start()

    def send_inside(c):
        for copy, edge in zip(halo(c), (3, 0)):
            pl.when(gram.x != edge)(copy.start)

    def send_around(c):
        for copy, edge in zip(halo(c), (3, 0)):
            pl.when(gram.x == edge)(copy.start)

    def pot_halo():
        return [
            remote(pot, pots.at[0], pot_s.at[0], pot_r.at[0], {"dom": right}),
            remote(pot, pots.at[2], pot_s.at[1], pot_r.at[1], {"dom": left}),
        ]

    for copy in pot_halo():
        copy.start()
    for c in range(EARLY):
        send_halo(c)
    mine = [pltpu.make_async_copy(orb, own, local.at[0]), pltpu.make_async_copy(pot, pots.at[1], local.at[1])]
    for copy in mine:
        copy.start()
    for copy in mine:
        copy.wait()
    for copy in pot_halo():
        copy.wait_recv()

    flat = ym.reshape(16 * ROWS, 128)

    def run_filter(c):
        begin, count = CHUNKS[c]
        for copy in halo(c):
            copy.wait_recv()
        potential = [pots[j // 2, j % 2] for j in range(6)]

        def some(i, _):
            for step in range(TOGETHER):
                o = begin + TOGETHER * i + step
                v = [left_in[o, 0], left_in[o, 1], own[o, 0], own[o, 1], right_in[o, 0], right_in[o, 1]]
                for plane, value in enumerate(filtered(v, potential)):
                    flat[pl.ds(plane * 8 * ROWS + o, 8, stride=ROWS), :] = value
            return 0

        lax.fori_loop(0, count // TOGETHER, some, 0)

    def y_copy(c):
        rows = pl.ds(*CHUNKS[c])
        return pltpu.make_async_copy(ym.at[:, rows], y_out.at[:, rows], local.at[2 + c])

    def panel_rows(p, half):
        return pm.at[:, pl.ds(p * PANEL + half * 32, 32)]

    def owner_copies(p, half):
        rows = ym.at[:, pl.ds(half * 32, 32)]
        targets = [p ^ 1, (p + 2) % BAND, (p + 4) % BAND, (p + 6) % BAND]
        return [
            remote(rows, panel_rows(p, half), pan_s.at[half, k], pan_r.at[p, half], {"band": t})
            for k, t in enumerate(targets)
        ]

    def relay_copy(p, half):
        ref = panel_rows(p, half)
        return remote(ref, ref, relay_s.at[p, half], pan_r.at[p, half], {"band": band + 1 - 2 * core})

    def relays(p):
        return (core == p % 2) & (y != p // 2)

    def send_panel(half):
        for p in range(PANELS):

            @pl.when(band == p)
            def _():
                for copy in owner_copies(p, half):
                    copy.start()
                begin, count = CHUNKS[half]
                pm[:, p * PANEL + begin : p * PANEL + begin + count] = ym[:, begin : begin + count]

    def take_panel(half):
        for p in range(PANELS):

            @pl.when(band != p)
            def _():
                relay_copy(p, half).wait_recv()

            @pl.when(relays(p))
            def _():
                relay_copy(p, half).start()

    def inner(begin, count, total, at):
        def some(k, acc):
            a0, a1 = pieces(ym[k, begin : begin + count], 2)
            b0, b1 = ph[k], plo[k]
            both = mm_t(jnp.concatenate([a0, a1], axis=1), jnp.concatenate([b0, b0], axis=1))
            return acc + (both + mm_t(a0, b1))

        total.loc[at : at + count] = lax.fori_loop(0, 16, some, jnp.zeros((count, ALL), F32), unroll=16)

    run_filter(0)
    send_panel(0)
    run_filter(1)
    send_panel(1)
    take_panel(0)
    run_filter(2)
    y_copy(2).start()
    take_panel(1)

    p_copy = pltpu.make_async_copy(pm, p_out, local.at[2 + len(CHUNKS)])
    p_copy.start()

    def gram_step(k, acc):
        a0, a1 = pieces(pm[k], 2)
        ph[k] = a0
        plo[k] = a1
        return acc + (mm_t(a0, a0) + (mm_t(a0, a1) + mm_t(a1, a0)))

    gram.loc[...] = lax.fori_loop(0, 16, gram_step, jnp.zeros((ALL, ALL), F32), unroll=8)
    gram.start()
    send_halo(4)
    inner(0, 128, bulk, 0)
    gram.over_z()
    send_inside(5)
    for half in range(2):
        for p in range(PANELS):

            @pl.when(band == p)
            def _():
                for copy in owner_copies(p, half):
                    copy.wait_send()
                begin, count = CHUNKS[half]
                ym[:, begin : begin + count] = jnp.zeros((16, count, 128), F32)

        y_copy(half).start()
    run_filter(3)
    y_copy(3).start()
    send_inside(6)
    gram.over_x()
    send_inside(7)
    send_inside(8)
    gram.end()
    send_around(5)
    send_around(6)
    send_around(7)
    send_around(8)

    g = gram.full[...]
    eye = identity(PANEL)
    none = jnp.zeros((PANEL, PANEL), F32)
    t0 = jnp.concatenate([inv_sqrt(g[:PANEL, :PANEL]), none, none], axis=1)
    a = jnp.concatenate([jnp.concatenate([none, eye, none], axis=1), jnp.concatenate([none, none, eye], axis=1)], axis=0)
    a = a - exact(exact_t(g[PANEL:], t0), t0)
    ag = exact(a, g)
    s1 = exact_t(ag[:PANEL], a[:PANEL])
    for c in (4, 5, 6, 7):
        run_filter(c)
        y_copy(c).start()
    inner(128, 128, bulk, 128)
    bulk.start()
    root1 = inv_sqrt(s1)
    t1 = exact(root1, a[:PANEL])
    r1 = t1 - exact(exact_t(exact(root1, ag[:PANEL]), t0), t0)
    t01 = jnp.concatenate([t0, t1], axis=0)
    r01 = jnp.concatenate([t0, r1], axis=0)
    bulk.over_z()
    a2 = a[PANEL:] - exact(exact_t(ag[PANEL:], t1), t1)
    a2g = exact(a2, g)
    s2 = exact_t(a2g, a2)
    for c in (8,):
        run_filter(c)
        y_copy(c).start()
    inner(BULK, ROWS - BULK, last, 0)
    last.start()
    root2 = inv_sqrt(s2, (bulk.over_x, last.over_z, last.over_x))
    t2 = exact(root2, a2)
    before = exact_t(exact(root2, a2g), t01)
    bulk.end()
    t = jnp.concatenate([t01, t2], axis=0)
    r = jnp.concatenate([r01, t2 - exact(before, r01)], axis=0)
    d_out[:BULK] = exact(exact_t(bulk.full[...], r), t)
    for p, rows in enumerate((t0, t1, t2)):

        @pl.when(band == p)
        def _():
            d_out[:PANEL] = -rows

    last.end()
    d_out[BULK:] = exact(exact_t(last.full[...], r), t)

    for c in range(len(CHUNKS)):
        for copy in halo(c):
            copy.wait_send()
        y_copy(c).wait()
    for copy in pot_halo():
        copy.wait_send()
    for half in range(2):
        for p in range(PANELS):

            @pl.when(relays(p))
            def _():
                relay_copy(p, half).wait_send()

    p_copy.wait()
    for total in (gram, bulk, last):
        total.sent()


def project(orb, pot):
    scratch = [pltpu.VMEM((ROWS, 2, 8, 128), F32)] * 3 + [
        pltpu.VMEM((3, 2, 8, 128), F32),
        pltpu.VMEM((16, ROWS, 128), F32),
        pltpu.VMEM((16, ALL, 128), F32),
        pltpu.VMEM((16, ALL, 128), BF16),
        pltpu.VMEM((16, ALL, 128), BF16),
    ]
    scratch += sum_scratch(ALL) + sum_scratch(BULK) + sum_scratch(ROWS - BULK)
    scratch += [
        pltpu.SemaphoreType.DMA((2, len(CHUNKS))),
        pltpu.SemaphoreType.DMA((2, len(CHUNKS))),
        pltpu.SemaphoreType.DMA((2,)),
        pltpu.SemaphoreType.DMA((2,)),
        pltpu.SemaphoreType.DMA((2, 4)),
        pltpu.SemaphoreType.DMA((PANELS, 2)),
        pltpu.SemaphoreType.DMA((PANELS, 2)),
        pltpu.SemaphoreType.DMA((3 + len(CHUNKS),)),
    ]
    anywhere = pl.BlockSpec(memory_space=pltpu.HBM)
    return pl.pallas_call(
        body,
        out_shape=(
            jax.ShapeDtypeStruct((16, ROWS, 128), F32),
            jax.ShapeDtypeStruct((16, ALL, 128), F32),
            jax.ShapeDtypeStruct((ROWS, ALL), F32),
        ),
        in_specs=[anywhere, anywhere],
        out_specs=(anywhere, anywhere, pl.BlockSpec(memory_space=pltpu.VMEM)),
        scratch_shapes=scratch,
        compiler_params=pltpu.CompilerParams(collective_id=0, has_side_effects=True, vmem_limit_bytes=40 << 20),
        name="filter_and_project",
    )(orb, pot)


STEP = 160


def update_body(y, p, d, out, ph, plo):
    @pl.when(pl.program_id(0) == 0)
    def _():
        def cast(k, _):
            ph[k], plo[k] = pieces(p[k], 2)
            return 0

        lax.fori_loop(0, 16, cast, 0)

    d0, d1 = pieces(d[...], 2)
    flat = out.reshape(STEP * 16, 128)

    def some(k, _):
        rows = y[k] - (mm(d0, ph[k]) + (mm(d0, plo[k]) + mm(d1, ph[k])))
        for i in range(STEP // 8):
            flat[pl.ds(i * 128 + k, 8, stride=16), :] = rows[i * 8 : i * 8 + 8]
        return 0

    lax.fori_loop(0, 16, some, 0, unroll=8)


def update(y, p, d):
    return pl.pallas_call(
        update_body,
        grid=(ROWS // STEP,),
        out_shape=jax.ShapeDtypeStruct((ROWS, 2, 8, 128), F32),
        in_specs=[
            pl.BlockSpec((16, STEP, 128), lambda i: (0, i, 0)),
            pl.BlockSpec((16, ALL, 128), lambda i: (0, 0, 0), pipeline_mode=pl.Buffered(1)),
            pl.BlockSpec((STEP, ALL), lambda i: (i, 0)),
        ],
        out_specs=pl.BlockSpec((STEP, 2, 8, 128), lambda i: (i, 0, 0, 0)),
        scratch_shapes=[pltpu.VMEM((16, ALL, 128), BF16), pltpu.VMEM((16, ALL, 128), BF16)],
        compiler_params=pltpu.CompilerParams(vmem_limit_bytes=24 << 20),
        name="apply_update",
    )(y, p, d)


def per_device(orbitals, potential):
    return update(*project(orbitals, potential))


def solution(mesh):
    spec = P("band", "dom", None, None)
    return jax.shard_map(
        per_device, mesh=mesh, in_specs=(spec, P("dom", None, None)), out_specs=spec, check_vma=False
    )
```
